32 devices in a mesh: grp: 4 (over y, core), head: 8 (over z, x).
Axes of the slice: x: 2, y: 2, z: 4, core: 2. Of those that a mesh axis runs over, the one named last changes fastest.
Arguments:
- hidden_in: bfloat16 [96, 4096], P('grp', 'head'), may hold values from -6 to 6
- attention_gain: float32 [4096], replicated, may hold values from 0.1 to 1.9
- w_query: bfloat16 [4096, 4096], P(None, 'head'), may hold values from -0.09375 to 0.09375
- w_key_value: bfloat16 [2, 4096, 4096], P(None, None, 'head'), as said below
- w_attention_out: bfloat16 [4096, 4096], P('head'), may hold values from -0.09375 to 0.09375
- past_cache: bfloat16 [2, 96, 32, 128, 128], P(None, 'grp', 'head'), may hold values from -2000 to 2000, as said below
- lengths: int32 [96], P('grp'), may hold values from 2 to 128, as said below
- mamba_gain: float32 [4096], replicated, may hold values from 0.1 to 1.9
- w_in: bfloat16 [2, 4096, 8192], P(None, None, 'head'), may hold values from -0.09375 to 0.09375
- filter_weight: float32 [4, 8192], P(None, 'head'), may hold values from -3 to 3
- filter_bias: float32 [8192], P('head'), may hold values from -1.8 to 1.8
- filter_state: float32 [96, 3, 8192], P('grp', None, 'head'), may hold values from -6 to 6
- w_select: bfloat16 [8192, 288], P('head'), may hold values from -0.0625 to 0.0625
- w_step: bfloat16 [256, 8192], P(None, 'head'), may hold values from -0.375 to 0.375
- step_bias: float32 [8192], P('head'), may hold values from -4 to -1
- log_rate: float32 [16, 8192], P(None, 'head'), may hold values from 0 to 2.77
- skip_gain: float32 [8192], P('head'), may hold values from 0.1 to 1.9
- scan_state: float32 [96, 16, 8192], P('grp', None, 'head'), may hold values from -6 to 6
- w_mamba_out: bfloat16 [8192, 4096], P('head'), may hold values from -0.0625 to 0.0625
- reward_terms: float32 [96, 128], P('grp', 'head'), may hold values from -60 to 60
- reward_mask: int32 [96, 128], P('grp', 'head'), may hold values 0 or 1
Outputs:
- hidden_out: bfloat16 [96, 4096], P('grp', 'head')
- new_key_value: bfloat16 [2, 96, 32, 128], P(None, 'grp', 'head')
- new_filter_state: float32 [96, 3, 8192], P('grp', None, 'head')
- new_scan_state: float32 [96, 16, 8192], P('grp', None, 'head')
- rewards: float32 [96], P('grp')
The draws below stay inside these ranges and needn't reach their ends.
Inputs may be any that keep to these rules, and one draw needn't show every extreme that they name: `w_key_value`: query heads that share a key-value head (4 of them in a row) hold equal copies. `past_cache`: query heads that share a key-value head (4 of them in a row) hold equal copies. `lengths`: the first sample's cache is full (128).
All inputs are finite; a program needn't handle non-finite values. No bound on the sum of `reward_mask` on one device may be relied on, other than what follows from the above.
Results may differ from the reference program's by a relative error of at most 0.012.
Values may be sent and summed in bfloat16 or wider, within the bound.
No kernel may reach another device: no remote copies, remote signals or barrier semaphores. Data moves between devices by JAX's collectives and lax.ppermute only.
A program may use at most 128 MiB of HBM per device.

```python
import math
import jax
import jax.numpy as jnp
from jax import lax

D = 4096
HEADS = 32
KVH = 8
DH = 128
INNER = 8192
NSTATE = 16
CONV = 4
RANK = 256
CTX = 128
BATCH = 96


def draw_w_key_value(key, part):
    drawn = jax.random.normal(key, (2, D, KVH, DH), jnp.float32) * D ** (-0.5)
    copies = jnp.repeat(drawn, HEADS // KVH, axis=2)
    return copies.reshape(2, D, HEADS * DH).astype(jnp.bfloat16)


def draw_past_cache(key, part):
    base_key = jax.random.fold_in(key, 0)
    drawn = jnp.clip(jax.random.normal(base_key, (2, BATCH, KVH, CTX, DH), jnp.float32), -6.0, 6.0)
    return jnp.repeat(drawn, HEADS // KVH, axis=2).astype(jnp.bfloat16)


def draw_lengths(key, part):
    drawn = jax.random.randint(key, (BATCH,), 2, CTX + 1, dtype=jnp.int32)
    return drawn.at[0].set(CTX)


def draw_reward_terms(key, part):
    noise_key = jax.random.fold_in(key, 0)
    ramp = 1.0 + 2.0 * jnp.arange(CTX, dtype=jnp.float32) / (CTX - 1)
    noise = jnp.clip(jax.random.normal(noise_key, (BATCH, CTX), jnp.float32), -6.0, 6.0)
    return noise * ramp[None, :]


def plant(result, key, least, largest):
    shape = result.shape
    place = [jax.random.randint(jax.random.fold_in(key, axis), (), 0, shape[axis]) for axis in range(len(shape))]
    result = result.at[tuple(place)].set(least)
    longest = shape.index(max(shape))
    place[longest] = (place[longest] + 1) % shape[longest]
    return result.at[tuple(place)].set(largest)


def block_levels(own_key, extent, shards, low, high):
    def one(position, shards_of):
        steps = jax.random.uniform(jax.random.fold_in(jax.random.fold_in(own_key, 6), position), (shards_of,), jnp.float32, low / len(shards), high / len(shards))
        return jnp.repeat(jnp.exp(steps), extent[position] // shards_of).reshape((-1,) + (1,) * (len(extent) - position - 1))

    level = one(*shards[0])
    for cut in shards[1:]:
        level = level * one(*cut)
    return level


def bell_draw(stream_key, shape, width, limit, cuts=(), held_as=jnp.bfloat16):
    level = block_levels(stream_key, shape, cuts, -0.22, 0.18) if cuts else 1.0
    array = jax.random.normal(stream_key, shape, jnp.float32) * width * level
    return jnp.minimum(jnp.maximum(array, -limit), limit).astype(held_as)


def setup_inputs(seed: int = 0) -> dict:
    key_of = jax.random.split(jax.random.key(seed), 22)
    return {
        "hidden_in": bell_draw(key_of[0], (BATCH, D), 1.0, 6.0, ((0, 4), (1, 8))),
        "attention_gain": jnp.clip(1.0 + 0.18 * jax.random.normal(key_of[1], (D,), jnp.float32), 0.1, 1.9),
        "w_query": bell_draw(key_of[2], (D, HEADS * DH), D ** -0.5, 0.09375, ((1, 8),)),
        "w_key_value": draw_w_key_value(jax.random.fold_in(key_of[21], 71), 0),
        "w_attention_out": bell_draw(key_of[4], (HEADS * DH, D), (HEADS * DH) ** -0.5, 0.09375, ((0, 8),)),
        "past_cache": draw_past_cache(jax.random.fold_in(key_of[21], 71), 0),
        "lengths": draw_lengths(jax.random.fold_in(key_of[21], 71), 0),
        "mamba_gain": jnp.clip(1.0 + 0.18 * jax.random.normal(key_of[7], (D,), jnp.float32), 0.1, 1.9),
        "w_in": bell_draw(key_of[8], (2, D, INNER), D ** -0.5, 0.09375, ((2, 8),)),
        "filter_weight": bell_draw(key_of[9], (CONV, INNER), CONV ** -0.5, 3.0, ((1, 8),), jnp.float32),
        "filter_bias": bell_draw(key_of[10], (INNER,), 0.3, 1.8, ((0, 8),), jnp.float32),
        "filter_state": bell_draw(key_of[11], (BATCH, CONV - 1, INNER), 1.0, 6.0, ((0, 4), (2, 8)), jnp.float32),
        "w_select": bell_draw(key_of[12], (INNER, RANK + 2 * NSTATE), INNER ** -0.5, 0.0625, ((0, 8),)),
        "w_step": bell_draw(key_of[13], (RANK, INNER), RANK ** -0.5, 0.375, ((1, 8),)),
        "step_bias": jnp.clip(-4.0 + 3.0 * jax.random.uniform(key_of[14], (INNER,), jnp.float32) ** block_levels(key_of[14], (INNER,), ((0, 8),), -0.2, 0.2), -4.0, -1.0),
        "log_rate": jnp.clip(2.77 * jax.random.uniform(key_of[15], (NSTATE, INNER), jnp.float32) ** block_levels(key_of[15], (NSTATE, INNER), ((1, 8),), -0.2, 0.2), 0.0, 2.77),
        "skip_gain": jnp.clip(1.0 + 0.18 * jax.random.normal(key_of[16], (INNER,), jnp.float32), 0.1, 1.9),
        "scan_state": bell_draw(key_of[17], (BATCH, NSTATE, INNER), 1.0, 6.0, ((0, 4), (2, 8)), jnp.float32),
        "w_mamba_out": bell_draw(key_of[18], (INNER, D), INNER ** -0.5, 0.0625, ((0, 8),)),
        "reward_terms": draw_reward_terms(jax.random.fold_in(key_of[21], 71), 0),
        "reward_mask": plant((jax.random.randint(key_of[20], (BATCH, CTX), 0, 2) < 1).astype(jnp.int32), jax.random.fold_in(key_of[20], 1), 0, 1),
    }


EPS = 1e-06

def norm_rows(row_values, gain):
    values = row_values.astype(jnp.float32)
    factor = lax.rsqrt(lax.optimization_barrier(jnp.mean(values * values, axis=-1, keepdims=True)) + EPS)
    return (values * factor * gain).astype(jnp.bfloat16)

def attend_sample(query, cache, fresh, length):
    inv_root = 1.0 / math.sqrt(query.shape[-1])
    query_wide = query.astype(jnp.float32)
    scores = jnp.einsum('hd,htd->ht', query_wide, cache[0].astype(jnp.float32)) * inv_root
    positions = jnp.arange(cache.shape[2], dtype=jnp.int32)
    scores = jnp.where(positions[None, :] < length, scores, -jnp.inf)
    own_score = lax.optimization_barrier(jnp.sum(query_wide * fresh[0].astype(jnp.float32), axis=-1)) * inv_root
    row_max = jnp.maximum(lax.optimization_barrier(jnp.max(scores, axis=-1)), own_score)
    weights = jnp.exp(scores - row_max[:, None])
    own_weight = jnp.exp(own_score - row_max)
    denominator = lax.optimization_barrier(jnp.sum(weights, axis=-1)) + own_weight
    weights = (weights / denominator[:, None]).astype(jnp.bfloat16)
    own_weight = (own_weight / denominator).astype(jnp.bfloat16)
    blended = jnp.einsum('ht,htd->hd', weights.astype(jnp.float32), cache[1].astype(jnp.float32))
    blended = blended + own_weight.astype(jnp.float32)[:, None] * fresh[1].astype(jnp.float32)
    return blended.astype(jnp.bfloat16)

def reference(hidden_in, attention_gain, w_query, w_key_value, w_attention_out, past_cache, lengths, mamba_gain, w_in, filter_weight, filter_bias, filter_state, w_select, w_step, step_bias, log_rate, skip_gain, scan_state, w_mamba_out, reward_terms, reward_mask):
    normed = norm_rows(hidden_in, attention_gain)
    queries = jnp.dot(normed, w_query, preferred_element_type=jnp.float32).astype(jnp.bfloat16)
    queries = queries.reshape(BATCH, HEADS, DH)
    fresh_all = jnp.einsum('bd,kdc->kbc', normed.astype(jnp.float32), w_key_value.astype(jnp.float32))
    new_key_value = fresh_all.astype(jnp.bfloat16).reshape(2, BATCH, HEADS, DH)

    def one_sample(index):
        cache = lax.dynamic_index_in_dim(past_cache, index, 1, keepdims=False)
        fresh = lax.dynamic_index_in_dim(new_key_value, index, 1, keepdims=False)
        query = lax.dynamic_index_in_dim(queries, index, 0, keepdims=False)
        length = lax.dynamic_index_in_dim(lengths, index, 0, keepdims=False)
        return attend_sample(query, cache, fresh, length)
    attended = lax.map(one_sample, jnp.arange(BATCH, dtype=jnp.int32)).reshape(BATCH, HEADS * DH)
    head_terms = jnp.dot(attended, w_attention_out, preferred_element_type=jnp.float32)
    mixed = (hidden_in.astype(jnp.float32) + head_terms).astype(jnp.bfloat16)
    normed_two = norm_rows(mixed, mamba_gain)
    x_inner = jnp.dot(normed_two, w_in[0], preferred_element_type=jnp.float32)
    gate_part = jnp.dot(normed_two, w_in[1], preferred_element_type=jnp.float32)
    conv_sum = filter_bias + x_inner * filter_weight[CONV - 1]
    for tap_index in range(CONV - 1):
        conv_sum = conv_sum + filter_state[:, tap_index, :] * filter_weight[tap_index]
    conv_out = jax.nn.silu(conv_sum).astype(jnp.bfloat16)
    new_filter_state = jnp.concatenate([filter_state[:, 1:, :], x_inner[:, None, :]], axis=1)
    projected = jnp.dot(conv_out, w_select, preferred_element_type=jnp.float32)
    step_low = projected[:, :RANK].astype(jnp.bfloat16)
    b_input = projected[:, RANK:RANK + NSTATE]
    c_output = projected[:, RANK + NSTATE:]
    step_size = jax.nn.softplus(jnp.dot(step_low, w_step, preferred_element_type=jnp.float32) + step_bias)
    conv_value = conv_out.astype(jnp.float32)
    decay_rate = jnp.exp(-step_size[:, None, :] * jnp.exp(log_rate)[None, :, :])
    new_scan_state = decay_rate * scan_state + step_size[:, None, :] * b_input[:, :, None] * conv_value[:, None, :]
    scan_out = (lax.optimization_barrier(jnp.sum(c_output[:, :, None] * new_scan_state, axis=1)) + skip_gain * conv_value) * jax.nn.silu(gate_part)
    scan_out = scan_out.astype(jnp.bfloat16)
    hidden_out = (mixed.astype(jnp.float32) + jnp.dot(scan_out, w_mamba_out, preferred_element_type=jnp.float32)).astype(jnp.bfloat16)
    positions = jnp.arange(CTX, dtype=jnp.int32)
    live = (reward_mask == 1) & (positions[None, :] < lengths[:, None])
    rewards = lax.optimization_barrier(jnp.sum(jnp.where(live, reward_terms, 0.0), axis=1))
    return (hidden_out, new_key_value, new_filter_state, new_scan_state, rewards)
```

```python
import math

import jax
import jax.numpy as jnp
from jax import lax
from jax.sharding import PartitionSpec as P

EPS = 1e-06


def norm_rows(row_values, gain):
    values = row_values.astype(jnp.float32)
    factor = lax.rsqrt(jnp.mean(values * values, axis=-1, keepdims=True) + EPS)
    return (values * factor * gain).astype(jnp.bfloat16)


SHARED = 4


def exchange(parts):
    return lax.all_to_all(parts, "head", 0, 0)


def spread(block):
    peers = lax.axis_size("head")
    return exchange(jnp.broadcast_to(block[None], (peers,) + block.shape))


def add_scattered(terms):
    peers = lax.axis_size("head")
    rows, width = terms.shape
    parts = terms.astype(jnp.bfloat16).reshape(rows, peers, width // peers)
    received = exchange(jnp.transpose(parts, (1, 0, 2)))
    return jnp.sum(received.astype(jnp.float32), axis=0)


def side_by_side(blocks):
    peers, rows, width = blocks.shape
    return jnp.transpose(blocks, (1, 0, 2)).reshape(rows, peers * width)


def split_float(value):
    high = value.astype(jnp.bfloat16)
    rest = value - high.astype(jnp.float32)
    middle = rest.astype(jnp.bfloat16)
    low = (rest - middle.astype(jnp.float32)).astype(jnp.bfloat16)
    return jnp.stack([high, middle, low], axis=1)


def attend_block(queries, keys, values, fresh, lengths):
    inv_root = 1.0 / math.sqrt(queries.shape[-1])
    scores = (
        jnp.einsum("bgqd,bgtd->bgqt", queries, keys, preferred_element_type=jnp.float32) * inv_root
    )
    positions = lax.iota(jnp.int32, keys.shape[2])
    live = positions[None, None, None, :] < lengths[:, None, None, None]
    scores = jnp.where(live, scores, -jnp.inf)
    own_score = (
        jnp.sum(
            queries.astype(jnp.float32) * fresh[0].astype(jnp.float32)[:, :, None, :], axis=-1
        )
        * inv_root
    )
    row_max = jnp.maximum(jnp.max(scores, axis=-1), own_score)
    weights = jnp.exp(scores - row_max[..., None])
    own_weight = jnp.exp(own_score - row_max)
    denominator = jnp.sum(weights, axis=-1) + own_weight
    weights = (weights / denominator[..., None]).astype(jnp.bfloat16)
    own_weight = (own_weight / denominator).astype(jnp.bfloat16)
    blended = jnp.einsum("bgqt,bgtd->bgqd", weights, values, preferred_element_type=jnp.float32)
    blended = (
        blended
        + own_weight.astype(jnp.float32)[..., None]
        * fresh[1].astype(jnp.float32)[:, :, None, :]
    )
    return blended.astype(jnp.bfloat16)


def reward_partial(reward_terms, reward_mask, lengths):
    columns = reward_terms.shape[1]
    positions = lax.axis_index("head") * columns + lax.iota(jnp.int32, columns)
    live = (reward_mask == 1) & (positions[None, :] < lengths[:, None])
    return jnp.sum(jnp.where(live, reward_terms, 0.0), axis=1)


def local(
    hidden_in,
    attention_gain,
    w_query,
    w_key_value,
    w_attention_out,
    past_cache,
    lengths,
    mamba_gain,
    w_in,
    filter_weight,
    filter_bias,
    filter_state,
    w_select,
    w_step,
    step_bias,
    log_rate,
    skip_gain,
    scan_state,
    w_mamba_out,
    reward_terms,
    reward_mask,
):
    samples = hidden_in.shape[0]
    local_heads = past_cache.shape[2]
    head_size = past_cache.shape[4]
    rank_width = w_step.shape[0]
    state_width = log_rate.shape[0]
    copies = math.gcd(SHARED, local_heads)
    kv_heads = local_heads // copies
    peers = lax.axis_size("head")
    full_in = side_by_side(spread(hidden_in))
    normed = norm_rows(full_in, attention_gain)
    queries = jnp.dot(normed, w_query, preferred_element_type=jnp.float32).astype(jnp.bfloat16)
    queries = queries.reshape(samples, kv_heads, copies, head_size)
    group_width = copies * head_size
    w_single = jnp.concatenate(
        [
            w_key_value[:, :, group * group_width : group * group_width + head_size]
            for group in range(kv_heads)
        ],
        axis=2,
    )
    fresh_all = jnp.stack(
        [jnp.dot(normed, w_single[side], preferred_element_type=jnp.float32) for side in range(2)]
    )
    fresh = fresh_all.astype(jnp.bfloat16).reshape(2, samples, kv_heads, head_size)
    new_key_value = jnp.broadcast_to(
        fresh[:, :, :, None, :], (2, samples, kv_heads, copies, head_size)
    ).reshape(2, samples, local_heads, head_size)
    keys = past_cache[0, :, ::copies]
    values = past_cache[1, :, ::copies]
    attended = attend_block(queries, keys, values, fresh, lengths)
    attended = attended.reshape(samples, local_heads * head_size)
    head_terms = jnp.dot(attended, w_attention_out, preferred_element_type=jnp.float32)
    mixed = (hidden_in.astype(jnp.float32) + add_scattered(head_terms)).astype(jnp.bfloat16)
    mixed_full = side_by_side(spread(mixed))
    normed_two = norm_rows(mixed_full, mamba_gain)
    x_inner = jnp.dot(normed_two, w_in[0], preferred_element_type=jnp.float32)
    gate = jax.nn.silu(jnp.dot(normed_two, w_in[1], preferred_element_type=jnp.float32))
    gate = lax.optimization_barrier(gate)
    taps = filter_weight.shape[0]
    conv_sum = filter_bias + x_inner * filter_weight[taps - 1]
    for tap_index in range(taps - 1):
        conv_sum = conv_sum + filter_state[:, tap_index, :] * filter_weight[tap_index]
    conv_out = jax.nn.silu(conv_sum).astype(jnp.bfloat16)
    new_filter_state = jnp.concatenate([filter_state[:, 1:, :], x_inner[:, None, :]], axis=1)
    local_select = jnp.dot(conv_out, w_select, preferred_element_type=jnp.float32)
    reward_columns = split_float(reward_partial(reward_terms, reward_mask, lengths))
    sent = jnp.concatenate([local_select.astype(jnp.bfloat16), reward_columns], axis=1)
    totals = jnp.sum(spread(sent).astype(jnp.float32), axis=0)
    select_width = w_select.shape[1]
    projected = totals[:, :select_width]
    rewards = jnp.sum(totals[:, select_width:], axis=1)
    step_low = projected[:, :rank_width].astype(jnp.bfloat16)
    b_input = projected[:, rank_width : rank_width + state_width]
    c_output = projected[:, rank_width + state_width :]
    step_size = jax.nn.softplus(
        jnp.dot(step_low, w_step, preferred_element_type=jnp.float32) + step_bias
    )
    conv_value = conv_out.astype(jnp.float32)
    decay_rate = jnp.exp(-step_size[:, None, :] * jnp.exp(log_rate)[None, :, :])
    new_scan_state = (
        decay_rate * scan_state
        + step_size[:, None, :] * b_input[:, :, None] * conv_value[:, None, :]
    )
    scan_out = (
        jnp.sum(c_output[:, :, None] * new_scan_state, axis=1) + skip_gain * conv_value
    ) * gate
    scan_out = scan_out.astype(jnp.bfloat16)
    channel_terms = jnp.dot(scan_out, w_mamba_out, preferred_element_type=jnp.float32)
    mamba_sum = add_scattered(channel_terms)
    hidden_out = (mixed.astype(jnp.float32) + mamba_sum).astype(jnp.bfloat16)
    return (hidden_out, new_key_value, new_filter_state, new_scan_state, rewards)


def solution(mesh):
    placed = (
        P("grp", "head"),
        P(),
        P(None, "head"),
        P(None, None, "head"),
        P("head", None),
        P(None, "grp", "head", None, None),
        P("grp"),
        P(),
        P(None, None, "head"),
        P(None, "head"),
        P("head"),
        P("grp", None, "head"),
        P("head", None),
        P(None, "head"),
        P("head"),
        P(None, "head"),
        P("head"),
        P("grp", None, "head"),
        P("head", None),
        P("grp", "head"),
        P("grp", "head"),
    )
    return jax.shard_map(
        local,
        mesh=mesh,
        in_specs=placed,
        out_specs=(
            P("grp", "head"),
            P(None, "grp", "head", None),
            P("grp", None, "head"),
            P("grp", None, "head"),
            P("grp"),
        ),
        check_vma=False,
    )
```
